32 devices in a mesh: seq: 8 (over z, x), fsdp: 4 (over y, core).
Axes of the slice: x: 2, y: 2, z: 4, core: 2. Of those that a mesh axis runs over, the one named last changes fastest.
Arguments:
- tokens: bfloat16 [4, 1024, 1152], P('fsdp', 'seq'), may hold values from -6 to 6
- cotangent: bfloat16 [4, 1024, 1152], P('fsdp', 'seq'), may hold values from -6 to 6
- attn_norm: bfloat16 [1152], P('fsdp'), may hold values from 0.25 to 1.75
- q_norm: bfloat16 [256], P('fsdp'), may hold values from 0.25 to 1.75
- k_norm: bfloat16 [256], P('fsdp'), may hold values from 0.25 to 1.75
- post_attn_norm: bfloat16 [1152], P('fsdp'), may hold values from 0.25 to 1.75
- ffn_norm: bfloat16 [1152], P('fsdp'), may hold values from 0.25 to 1.75
- post_ffn_norm: bfloat16 [1152], P('fsdp'), may hold values from 0.25 to 1.75
- w_query: bfloat16 [1152, 1024], P('fsdp'), may hold values from -0.1875 to 0.1875
- w_key: bfloat16 [1152, 256], P('fsdp'), may hold values from -0.1875 to 0.1875
- w_value: bfloat16 [1152, 256], P('fsdp'), may hold values from -0.1875 to 0.1875
- w_out: bfloat16 [1024, 1152], P('fsdp'), may hold values from -0.1875 to 0.1875
- w_gate: bfloat16 [1152, 6912], P('fsdp'), may hold values from -0.1875 to 0.1875
- w_up: bfloat16 [1152, 6912], P('fsdp'), may hold values from -0.1875 to 0.1875
- w_down: bfloat16 [6912, 1152], P('fsdp'), may hold values from -0.078125 to 0.078125
Outputs:
- layer_out: bfloat16 [4, 1024, 1152], P('fsdp', 'seq')
- grad_tokens: float32 [4, 1024, 1152], P('fsdp', 'seq')
- grad_attn_norm: float32 [1152], P(('seq', 'fsdp'))
- grad_q_norm: float32 [256], P(('seq', 'fsdp'))
- grad_k_norm: float32 [256], P(('seq', 'fsdp'))
- grad_post_attn_norm: float32 [1152], P(('seq', 'fsdp'))
- grad_ffn_norm: float32 [1152], P(('seq', 'fsdp'))
- grad_post_ffn_norm: float32 [1152], P(('seq', 'fsdp'))
- grad_w_query: float32 [1152, 1024], P(('seq', 'fsdp'))
- grad_w_key: float32 [1152, 256], P(('seq', 'fsdp'))
- grad_w_value: float32 [1152, 256], P(('seq', 'fsdp'))
- grad_w_out: float32 [1024, 1152], P(None, ('seq', 'fsdp'))
- grad_w_gate: float32 [1152, 6912], P(('seq', 'fsdp'))
- grad_w_up: float32 [1152, 6912], P(('seq', 'fsdp'))
- grad_w_down: float32 [6912, 1152], P(None, ('seq', 'fsdp'))
The draws below stay inside these ranges and needn't reach their ends.
All inputs are finite; a program needn't handle non-finite values.
Results may differ from the reference program's by a relative error of at most 0.019.
Values may be sent and summed in bfloat16 or wider, within the bound.
A program may use at most 448 MiB of HBM per device.

```python
import jax
import jax.numpy as jnp
from jax import lax

D = 1152
HQ = 4
HD = 256
FF = 6912
W = 512
TOK_DEV = 128
SEQ_LEN = 1024
SEQS = 4


def levels(stream_key, shape, split, smallest, high):
    def one(dim, shards_of):
        steps = jax.random.uniform(jax.random.fold_in(jax.random.fold_in(stream_key, 6), dim), (shards_of,), jnp.float32, smallest / len(split), high / len(split))
        return jnp.repeat(jnp.exp(steps), shape[dim] // shards_of).reshape((-1,) + (1,) * (len(shape) - dim - 1))

    loudness = one(*split[0])
    for cut in split[1:]:
        loudness = loudness * one(*cut)
    return loudness


def bell_draw(rng, dims, scale, bound, cuts=(), kind=jnp.bfloat16):
    drawn = scale * jax.random.normal(rng, dims, jnp.float32)
    if cuts:
        drawn = drawn * levels(rng, dims, cuts, -0.22, 0.18)
    return jnp.clip(drawn, -bound, bound).astype(kind)


def setup_inputs(seed: int = 0) -> dict:
    keys = jax.random.split(jax.random.key(seed), 16)
    tokens = bell_draw(keys[0], (SEQS, SEQ_LEN, D), 1.0, 6.0, ((0, 4), (1, 8)))
    cotangent = bell_draw(keys[1], (SEQS, SEQ_LEN, D), 1.0, 6.0, ((0, 4), (1, 8)))
    attn_norm = jnp.clip(1.0 + 0.15 * jax.random.normal(keys[2], (D,), jnp.float32), 0.25, 1.75).astype(jnp.bfloat16)
    q_norm = jnp.clip(1.0 + 0.15 * jax.random.normal(keys[3], (HD,), jnp.float32), 0.25, 1.75).astype(jnp.bfloat16)
    k_norm = jnp.clip(1.0 + 0.15 * jax.random.normal(keys[4], (HD,), jnp.float32), 0.25, 1.75).astype(jnp.bfloat16)
    post_attn_norm = jnp.clip(1.0 + 0.15 * jax.random.normal(keys[5], (D,), jnp.float32), 0.25, 1.75).astype(jnp.bfloat16)
    ffn_norm = jnp.clip(1.0 + 0.15 * jax.random.normal(keys[6], (D,), jnp.float32), 0.25, 1.75).astype(jnp.bfloat16)
    post_ffn_norm = jnp.clip(1.0 + 0.15 * jax.random.normal(keys[7], (D,), jnp.float32), 0.25, 1.75).astype(jnp.bfloat16)
    w_query = bell_draw(keys[8], (D, HQ * HD), D ** -0.5, 0.1875, ((0, 4),))
    w_key = bell_draw(keys[9], (D, HD), D ** -0.5, 0.1875, ((0, 4),))
    w_value = bell_draw(keys[10], (D, HD), D ** -0.5, 0.1875, ((0, 4),))
    w_out = bell_draw(keys[11], (HQ * HD, D), (HQ * HD) ** -0.5, 0.1875, ((0, 4),))
    w_gate = bell_draw(keys[12], (D, FF), D ** -0.5, 0.1875, ((0, 4),))
    w_up = bell_draw(keys[13], (D, FF), D ** -0.5, 0.1875, ((0, 4),))
    w_down = bell_draw(keys[14], (FF, D), FF ** -0.5, 0.078125, ((0, 4),))
    return {"tokens": tokens, "cotangent": cotangent, "attn_norm": attn_norm, "q_norm": q_norm, "k_norm": k_norm, "post_attn_norm": post_attn_norm, "ffn_norm": ffn_norm, "post_ffn_norm": post_ffn_norm, "w_query": w_query, "w_key": w_key, "w_value": w_value, "w_out": w_out, "w_gate": w_gate, "w_up": w_up, "w_down": w_down}


epsilon = 1e-06

def norm_forward(vector, gain_vec):
    factor = lax.rsqrt(lax.optimization_barrier(jnp.mean(vector * vector, axis=-1, keepdims=True)) + epsilon)
    normed = vector * factor
    return (normed * gain_vec, normed, factor)

def norm_backward(upstream, gain_vec, normed, factor):
    scaled = upstream * gain_vec
    grad_input = factor * (scaled - normed * lax.optimization_barrier(jnp.mean(scaled * normed, axis=-1, keepdims=True)))
    grad_gain = lax.optimization_barrier(jnp.sum((upstream * normed).reshape(-1, normed.shape[-1]), axis=0))
    return (grad_input, grad_gain)

def rope_tables(position, head_width):
    half_width = head_width // 2
    frequency = 10000.0 ** (-(jnp.arange(half_width).astype(jnp.float32) * (2.0 / head_width)))
    angles = position.astype(jnp.float32)[:, None] * frequency[None, :]
    return (jnp.cos(angles), jnp.sin(angles))

def rotate(vector, cos_table, sin_table):
    half_width = vector.shape[-1] // 2
    lead_half = vector[..., :half_width]
    tail_half = vector[..., half_width:]
    return jnp.concatenate([lead_half * cos_table - tail_half * sin_table, tail_half * cos_table + lead_half * sin_table], axis=-1)

def unrotate(upstream, cos_table, sin_table):
    half_width = upstream.shape[-1] // 2
    lead_half = upstream[..., :half_width]
    tail_half = upstream[..., half_width:]
    return jnp.concatenate([lead_half * cos_table + tail_half * sin_table, tail_half * cos_table - lead_half * sin_table], axis=-1)

def window_mask(query_pos, key_pos):
    distance = query_pos[:, None] - key_pos[None, :]
    return (distance >= 0) & (distance < W) & (key_pos[None, :] >= 0)

def score_rows(query_bf, key_window, query_pos, key_pos):
    scores = jnp.einsum('bhd,ld->hbl', query_bf.astype(jnp.float32), key_window.astype(jnp.float32)) * HD ** (-0.5)
    return jnp.where(window_mask(query_pos, key_pos)[None], scores, -1e+30)

def attend(query_bf, key_window, value_window, query_pos, key_pos):
    scores = score_rows(query_bf, key_window, query_pos, key_pos)
    row_peak = lax.optimization_barrier(jnp.max(scores, axis=-1, keepdims=True))
    row_total = lax.optimization_barrier(jnp.sum(jnp.exp(scores - row_peak), axis=-1, keepdims=True))
    log_total = row_peak + jnp.log(row_total)
    prob_bf = jnp.exp(scores - log_total).astype(jnp.bfloat16)
    mixed_rows = jnp.einsum('hbl,ld->bhd', prob_bf.astype(jnp.float32), value_window.astype(jnp.float32))
    return (mixed_rows, log_total[..., 0])

def attend_back(query_bf, key_window, value_window, query_pos, key_pos, mixed_rows, log_total, grad_mixed_bf):
    scores = score_rows(query_bf, key_window, query_pos, key_pos)
    prob_rows = jnp.exp(scores - log_total[..., None])
    prob_bf = prob_rows.astype(jnp.bfloat16)
    grad_upper = grad_mixed_bf.astype(jnp.float32)
    grad_values = jnp.einsum('hbl,bhd->ld', prob_bf.astype(jnp.float32), grad_upper)
    grad_probs = jnp.einsum('bhd,ld->hbl', grad_upper, value_window.astype(jnp.float32))
    row_delta = lax.optimization_barrier(jnp.sum(grad_upper * mixed_rows, axis=-1))
    grad_scores_bf = (prob_rows * (grad_probs - jnp.transpose(row_delta)[:, :, None]) * HD ** (-0.5)).astype(jnp.bfloat16)
    grad_queries = jnp.einsum('hbl,ld->bhd', grad_scores_bf.astype(jnp.float32), key_window.astype(jnp.float32))
    grad_keys = jnp.einsum('hbl,bhd->ld', grad_scores_bf.astype(jnp.float32), query_bf.astype(jnp.float32))
    return (grad_queries, grad_keys, grad_values)

def matmul(left_op, right_op):
    return jnp.dot(left_op, right_op, preferred_element_type=jnp.float32)

def one_sequence(tokens, cotangent, weights):
    attn_norm, q_norm, k_norm, post_attn_norm, ffn_norm, post_ffn_norm, w_query, w_key, w_value, w_out, w_gate, w_up, w_down = weights
    gain_attn = attn_norm.astype(jnp.float32)
    gain_query = q_norm.astype(jnp.float32)
    gain_key = k_norm.astype(jnp.float32)
    gain_post_attn = post_attn_norm.astype(jnp.float32)
    gain_ffn = ffn_norm.astype(jnp.float32)
    gain_post_ffn = post_ffn_norm.astype(jnp.float32)
    length = tokens.shape[0]
    block_rows = TOK_DEV
    block_count = length // block_rows
    residual = tokens.astype(jnp.float32)
    attn_scaled, attn_unit, attn_factor = norm_forward(residual, gain_attn)
    attn_in = attn_scaled.astype(jnp.bfloat16)
    query_raw = matmul(attn_in, w_query).reshape(length, HQ, HD)
    key_raw = matmul(attn_in, w_key)
    value_raw = matmul(attn_in, w_value)
    query_scaled, query_unit, query_factor = norm_forward(query_raw, gain_query)
    key_scaled, key_unit, key_factor = norm_forward(key_raw, gain_key)
    cos_table, sin_table = rope_tables(jnp.arange(length, dtype=jnp.int32), HD)
    query_bf = rotate(query_scaled, cos_table[:, None, :], sin_table[:, None, :]).astype(jnp.bfloat16)
    key_bf = rotate(key_scaled, cos_table, sin_table).astype(jnp.bfloat16)
    value_bf = value_raw.astype(jnp.bfloat16)
    pad_keys = jnp.concatenate([jnp.zeros((W, HD), jnp.bfloat16), key_bf], axis=0)
    pad_values = jnp.concatenate([jnp.zeros((W, HD), jnp.bfloat16), value_bf], axis=0)

    def block_view(number):
        row_start = (number * block_rows).astype(jnp.int32)
        query_block = lax.dynamic_slice_in_dim(query_bf, row_start, block_rows, 0)
        key_block = lax.dynamic_slice_in_dim(pad_keys, row_start, W + block_rows, 0)
        value_block = lax.dynamic_slice_in_dim(pad_values, row_start, W + block_rows, 0)
        query_pos = row_start + jnp.arange(block_rows, dtype=jnp.int32)
        key_pos = row_start - W + jnp.arange(W + block_rows, dtype=jnp.int32)
        return (row_start, query_block, key_block, value_block, query_pos, key_pos)

    def forward_block(number):
        row_start, query_block, key_block, value_block, query_pos, key_pos = block_view(number)
        return attend(query_block, key_block, value_block, query_pos, key_pos)
    numbers = jnp.arange(block_count, dtype=jnp.int32)
    mixed_blocks, log_blocks = lax.map(forward_block, numbers)
    mixed_bf = mixed_blocks.reshape(length, HQ * HD).astype(jnp.bfloat16)
    branch = matmul(mixed_bf, w_out)
    branch_out, branch_unit, branch_factor = norm_forward(branch, gain_post_attn)
    hidden = residual + branch_out
    ffn_scaled, ffn_unit, ffn_factor = norm_forward(hidden, gain_ffn)
    ffn_in = ffn_scaled.astype(jnp.bfloat16)
    gate_pre = matmul(ffn_in, w_gate)
    up_pre = matmul(ffn_in, w_up)
    gate_act = jax.nn.gelu(gate_pre, approximate=True)
    product_bf = (gate_act * up_pre).astype(jnp.bfloat16)
    down_pre = matmul(product_bf, w_down)
    down_out, down_unit, down_factor = norm_forward(down_pre, gain_post_ffn)
    layer_out = (hidden + down_out).astype(jnp.bfloat16)
    upstream = cotangent.astype(jnp.float32)
    grad_down, grad_post_ffn = norm_backward(upstream, gain_post_ffn, down_unit, down_factor)
    grad_down_bf = grad_down.astype(jnp.bfloat16)
    grad_w_down = matmul(product_bf.T, grad_down_bf)
    grad_product = matmul(grad_down_bf, w_down.T)
    grad_up_bf = (grad_product * gate_act).astype(jnp.bfloat16)
    unused_value, gelu_back = jax.vjp(lambda pre_act: jax.nn.gelu(pre_act, approximate=True), gate_pre)
    grad_gate_bf = gelu_back(grad_product * up_pre)[0].astype(jnp.bfloat16)
    grad_w_gate = matmul(ffn_in.T, grad_gate_bf)
    grad_w_up = matmul(ffn_in.T, grad_up_bf)
    grad_ffn_in = matmul(grad_gate_bf, w_gate.T) + matmul(grad_up_bf, w_up.T)
    grad_hidden_ffn, grad_ffn = norm_backward(grad_ffn_in, gain_ffn, ffn_unit, ffn_factor)
    grad_hidden = upstream + grad_hidden_ffn
    grad_branch, grad_post_attn = norm_backward(grad_hidden, gain_post_attn, branch_unit, branch_factor)
    grad_branch_bf = grad_branch.astype(jnp.bfloat16)
    grad_w_out = matmul(mixed_bf.T, grad_branch_bf)
    grad_mixed_bf = matmul(grad_branch_bf, w_out.T).astype(jnp.bfloat16)
    grad_blocks = grad_mixed_bf.reshape(block_count, block_rows, HQ, HD)

    def backward_block(running, inputs):
        grad_key_pad, grad_value_pad = running
        number, mixed_block, log_block, grad_block = inputs
        row_start, query_block, key_block, value_block, query_pos, key_pos = block_view(number)
        grad_queries, grad_keys, grad_values = attend_back(query_block, key_block, value_block, query_pos, key_pos, mixed_block, log_block, grad_block)
        grad_key_pad = lax.dynamic_update_slice_in_dim(grad_key_pad, lax.dynamic_slice_in_dim(grad_key_pad, row_start, W + block_rows, 0) + grad_keys, row_start, 0)
        grad_value_pad = lax.dynamic_update_slice_in_dim(grad_value_pad, lax.dynamic_slice_in_dim(grad_value_pad, row_start, W + block_rows, 0) + grad_values, row_start, 0)
        return ((grad_key_pad, grad_value_pad), grad_queries)
    start_pads = (jnp.zeros((W + length, HD), jnp.float32), jnp.zeros((W + length, HD), jnp.float32))
    (grad_key_pad, grad_value_pad), grad_query_blocks = lax.scan(backward_block, start_pads, (numbers, mixed_blocks, log_blocks, grad_blocks))
    grad_query_rot = grad_query_blocks.reshape(length, HQ, HD)
    grad_key_rot = grad_key_pad[W:]
    grad_value = grad_value_pad[W:]
    grad_query_raw, grad_q = norm_backward(unrotate(grad_query_rot, cos_table[:, None, :], sin_table[:, None, :]), gain_query, query_unit, query_factor)
    grad_key_raw, grad_k = norm_backward(unrotate(grad_key_rot, cos_table, sin_table), gain_key, key_unit, key_factor)
    grad_query_bf = grad_query_raw.reshape(length, HQ * HD).astype(jnp.bfloat16)
    grad_key_bf = grad_key_raw.astype(jnp.bfloat16)
    grad_value_bf = grad_value.astype(jnp.bfloat16)
    grad_w_query = matmul(attn_in.T, grad_query_bf)
    grad_w_key = matmul(attn_in.T, grad_key_bf)
    grad_w_value = matmul(attn_in.T, grad_value_bf)
    grad_attn_in = matmul(grad_query_bf, w_query.T) + matmul(grad_key_bf, w_key.T) + matmul(grad_value_bf, w_value.T)
    grad_residual, grad_attn = norm_backward(grad_attn_in, gain_attn, attn_unit, attn_factor)
    grad_tokens = grad_hidden + grad_residual
    grads = (grad_attn, grad_q, grad_k, grad_post_attn, grad_ffn, grad_post_ffn, grad_w_query, grad_w_key, grad_w_value, grad_w_out, grad_w_gate, grad_w_up, grad_w_down)
    return (layer_out, grad_tokens, grads)

def reference(tokens, cotangent, attn_norm, q_norm, k_norm, post_attn_norm, ffn_norm, post_ffn_norm, w_query, w_key, w_value, w_out, w_gate, w_up, w_down):
    weights = (attn_norm, q_norm, k_norm, post_attn_norm, ffn_norm, post_ffn_norm, w_query, w_key, w_value, w_out, w_gate, w_up, w_down)
    start_sums = jax.tree.map(lambda weight_arr: jnp.zeros(weight_arr.shape, jnp.float32), weights)

    def per_sequence(running, sequence_pair):
        layer_out, grad_tokens, grads = one_sequence(sequence_pair[0], sequence_pair[1], weights)
        summed = jax.tree.map(lambda total_arr, update: total_arr + update, running, grads)
        return (summed, (layer_out, grad_tokens))
    sums, (layer_out, grad_tokens) = lax.scan(per_sequence, start_sums, (tokens, cotangent))
    return (layer_out, grad_tokens, sums[0], sums[1], sums[2], sums[3], sums[4], sums[5], sums[6], sums[7], sums[8], sums[9], sums[10], sums[11], sums[12])
```

```python
import jax
import jax.numpy as jnp
from jax import lax
from jax.sharding import PartitionSpec as P

HQ = 4
HD = 256
W = 512


epsilon = 1e-06


def passed_along(value, axis, steps):
    count = lax.axis_size(axis)
    leading, last = (max(0, -steps), min(count, count - steps))
    return lax.ppermute(value, axis, [(source, source + steps) for source in range(leading, last)])


def norm_forward(vector, gain_vec):
    factor = lax.rsqrt(jnp.mean(vector * vector, axis=-1, keepdims=True) + epsilon)
    normed = vector * factor
    return (normed * gain_vec, normed, factor)


def norm_backward(upstream, gain_vec, normed, factor):
    scaled = upstream * gain_vec
    grad_input = factor * (scaled - normed * jnp.mean(scaled * normed, axis=-1, keepdims=True))
    grad_gain = jnp.sum((upstream * normed).reshape(-1, normed.shape[-1]), axis=0)
    return (grad_input, grad_gain)


def rope_tables(position, head_width):
    half_width = head_width // 2
    frequency = 10000.0 ** (-(jnp.arange(half_width).astype(jnp.float32) * (2.0 / head_width)))
    angles = position.astype(jnp.float32)[:, None] * frequency[None, :]
    return (jnp.cos(angles), jnp.sin(angles))


def rotate(vector, cos_table, sin_table):
    half_width = vector.shape[-1] // 2
    lead_half = vector[..., :half_width]
    tail_half = vector[..., half_width:]
    return jnp.concatenate(
        [
            lead_half * cos_table - tail_half * sin_table,
            tail_half * cos_table + lead_half * sin_table,
        ],
        axis=-1,
    )


def unrotate(upstream, cos_table, sin_table):
    half_width = upstream.shape[-1] // 2
    lead_half = upstream[..., :half_width]
    tail_half = upstream[..., half_width:]
    return jnp.concatenate(
        [
            lead_half * cos_table + tail_half * sin_table,
            tail_half * cos_table - lead_half * sin_table,
        ],
        axis=-1,
    )


def window_mask(query_pos, key_pos):
    distance = query_pos[:, None] - key_pos[None, :]
    return (distance >= 0) & (distance < W) & (key_pos[None, :] >= 0)


def score_rows(query_bf, key_window, query_pos, key_pos):
    scores = jnp.einsum(
        "bhd,ld->hbl", query_bf, key_window, preferred_element_type=jnp.float32
    ) * HD ** (-0.5)
    return jnp.where(window_mask(query_pos, key_pos)[None], scores, -1e30)


def attend(query_bf, key_window, value_window, query_pos, key_pos):
    scores = score_rows(query_bf, key_window, query_pos, key_pos)
    row_peak = jnp.max(scores, axis=-1, keepdims=True)
    row_total = jnp.sum(jnp.exp(scores - row_peak), axis=-1, keepdims=True)
    log_total = row_peak + jnp.log(row_total)
    prob_bf = jnp.exp(scores - log_total).astype(jnp.bfloat16)
    mixed_rows = jnp.einsum(
        "hbl,ld->bhd", prob_bf, value_window, preferred_element_type=jnp.float32
    )
    return (mixed_rows, log_total[..., 0])


def attend_back(
    query_bf, key_window, value_window, query_pos, key_pos, mixed_rows, log_total, grad_mixed_bf
):
    scores = score_rows(query_bf, key_window, query_pos, key_pos)
    prob_rows = jnp.exp(scores - log_total[..., None])
    prob_bf = prob_rows.astype(jnp.bfloat16)
    grad_values = jnp.einsum(
        "hbl,bhd->ld", prob_bf, grad_mixed_bf, preferred_element_type=jnp.float32
    )
    grad_probs = jnp.einsum(
        "bhd,ld->hbl", grad_mixed_bf, value_window, preferred_element_type=jnp.float32
    )
    row_delta = jnp.sum(grad_mixed_bf.astype(jnp.float32) * mixed_rows, axis=-1)
    grad_scores_bf = (
        prob_rows * (grad_probs - jnp.transpose(row_delta)[:, :, None]) * HD ** (-0.5)
    ).astype(jnp.bfloat16)
    grad_queries = jnp.einsum(
        "hbl,ld->bhd", grad_scores_bf, key_window, preferred_element_type=jnp.float32
    )
    grad_keys = jnp.einsum(
        "hbl,bhd->ld", grad_scores_bf, query_bf, preferred_element_type=jnp.float32
    )
    return (grad_queries, grad_keys, grad_values)


def matmul(left_op, right_op):
    return jnp.dot(left_op, right_op, preferred_element_type=jnp.float32)


def contract_rows(left_op, right_op):
    return lax.dot_general(
        left_op, right_op, (((0,), (0,)), ((), ())), preferred_element_type=jnp.float32
    )


def contract_cols(left_op, right_op):
    return lax.dot_general(
        left_op, right_op, (((1,), (1,)), ((), ())), preferred_element_type=jnp.float32
    )


def row_sums(partial):
    return lax.psum_scatter(
        partial.astype(jnp.bfloat16), "seq", scatter_dimension=0, tiled=True
    ).astype(jnp.float32)


def placed(rows, owned, padded, seq_size, fsdp_size):
    slot = jnp.arange(seq_size * fsdp_size * padded)
    block = slot // padded
    inner = slot % padded
    owner = (block % seq_size) * fsdp_size + block // seq_size
    source = jnp.where(inner < owned, owner * owned + inner, -1)
    pick = (jnp.arange(rows.shape[1])[:, None] == source[None, :]).astype(jnp.bfloat16)
    return matmul(rows, pick).astype(jnp.bfloat16)


def on_device(
    tokens,
    cotangent,
    attn_norm,
    q_norm,
    k_norm,
    post_attn_norm,
    ffn_norm,
    post_ffn_norm,
    w_query,
    w_key,
    w_value,
    w_out,
    w_gate,
    w_up,
    w_down,
):
    block_rows = tokens.shape[1]
    halo_rows = min(block_rows, W)
    halo_count = W // halo_rows
    seq_size = lax.axis_size("seq")
    fsdp_size = lax.axis_size("fsdp")
    owners = seq_size * fsdp_size
    seq_index = lax.axis_index("seq")
    width = tokens.shape[2]
    qkv_local = jnp.concatenate([w_query, w_key, w_value], axis=1)
    gains_local = (attn_norm, post_attn_norm, ffn_norm, post_ffn_norm, q_norm, k_norm)
    gain_row = jnp.concatenate(gains_local)
    gain_rows = jnp.pad(gain_row[None], ((0, 7), (0, qkv_local.shape[1] - gain_row.shape[0])))
    packed = lax.all_gather(jnp.concatenate([qkv_local, gain_rows], axis=0), "fsdp", axis=0)
    local_width = qkv_local.shape[0]
    w_qkv = packed[:, :local_width].reshape(width, -1)
    gain_all = packed[:, local_width].astype(jnp.float32)
    gains = []
    edge = 0
    for part in gains_local:
        gains.append(gain_all[:, edge : edge + part.shape[0]].reshape(-1))
        edge += part.shape[0]
    gain_attn, gain_post_attn, gain_ffn, gain_post_ffn, gain_query, gain_key = gains
    w_out_full = lax.all_gather(w_out, "fsdp", axis=0, tiled=True)
    ffn_block = w_down.shape[0]
    piece = ffn_block // seq_size
    slice_width = piece * fsdp_size

    def hidden_slice(weight):
        return jnp.concatenate(
            [
                lax.dynamic_slice_in_dim(weight, block * ffn_block + seq_index * piece, piece, 1)
                for block in range(fsdp_size)
            ],
            axis=1,
        )

    gate_up_local = jnp.stack([hidden_slice(w_gate), hidden_slice(w_up)])
    gate_up = lax.all_gather(gate_up_local, "fsdp", axis=0)
    w_gate_part = gate_up[:, 0].reshape(width, slice_width)
    w_up_part = gate_up[:, 1].reshape(width, slice_width)
    w_down_part = lax.all_gather(
        lax.dynamic_slice_in_dim(w_down, seq_index * piece, piece, 0), "fsdp", axis=0, tiled=True
    )
    base_row = lax.axis_index("seq") * block_rows
    query_pos = base_row + jnp.arange(block_rows, dtype=jnp.int32)
    key_pos = base_row - W + jnp.arange(W + block_rows, dtype=jnp.int32)
    cos_table, sin_table = rope_tables(query_pos, HD)
    residual = tokens[0].astype(jnp.float32)
    attn_scaled, attn_unit, attn_factor = norm_forward(residual, gain_attn)
    attn_in = attn_scaled.astype(jnp.bfloat16)
    query_width = HQ * HD
    qkv_raw = matmul(attn_in, w_qkv)
    query_raw = qkv_raw[:, :query_width].reshape(block_rows, HQ, HD)
    key_raw = qkv_raw[:, query_width : query_width + HD]
    value_raw = qkv_raw[:, query_width + HD :]
    query_scaled, query_unit, query_factor = norm_forward(query_raw, gain_query)
    key_scaled, key_unit, key_factor = norm_forward(key_raw, gain_key)
    query_bf = rotate(query_scaled, cos_table[:, None, :], sin_table[:, None, :]).astype(
        jnp.bfloat16
    )
    key_bf = rotate(key_scaled, cos_table, sin_table).astype(jnp.bfloat16)
    value_bf = value_raw.astype(jnp.bfloat16)
    both_bf = jnp.concatenate([key_bf, value_bf], axis=1)
    both_parts = [passed_along(both_bf, "seq", offset) for offset in range(halo_count, 0, -1)]
    both_window = jnp.concatenate(both_parts + [both_bf], axis=0)
    key_window = both_window[:, :HD]
    value_window = both_window[:, HD:]
    mixed_rows, log_total = attend(query_bf, key_window, value_window, query_pos, key_pos)
    mixed_bf = mixed_rows.reshape(block_rows, HQ * HD).astype(jnp.bfloat16)
    branch = matmul(mixed_bf, w_out_full)
    branch_out, branch_unit, branch_factor = norm_forward(branch, gain_post_attn)
    hidden = residual + branch_out
    ffn_scaled, ffn_unit, ffn_factor = norm_forward(hidden, gain_ffn)
    ffn_in = lax.all_gather(ffn_scaled.astype(jnp.bfloat16), "seq", axis=0, tiled=True)
    gate_pre = matmul(ffn_in, w_gate_part)
    up_pre = matmul(ffn_in, w_up_part)
    gate_act = jax.nn.gelu(gate_pre, approximate=True)
    product_bf = (gate_act * up_pre).astype(jnp.bfloat16)
    down_pre = row_sums(matmul(product_bf, w_down_part))
    down_out, down_unit, down_factor = norm_forward(down_pre, gain_post_ffn)
    layer_out = (hidden + down_out).astype(jnp.bfloat16)
    upstream = cotangent[0].astype(jnp.float32)
    grad_down, grad_post_ffn = norm_backward(upstream, gain_post_ffn, down_unit, down_factor)
    grad_down_bf = lax.all_gather(grad_down.astype(jnp.bfloat16), "seq", axis=0, tiled=True)
    grad_product = contract_cols(grad_down_bf, w_down_part)
    grad_up_bf = (grad_product * gate_act).astype(jnp.bfloat16)
    unused_value, gelu_back = jax.vjp(
        lambda pre_act: jax.nn.gelu(pre_act, approximate=True), gate_pre
    )
    grad_gate_bf = gelu_back(grad_product * up_pre)[0].astype(jnp.bfloat16)
    grad_ffn_part = (
        contract_cols(grad_gate_bf, w_gate_part) + contract_cols(grad_up_bf, w_up_part)
    ).astype(jnp.bfloat16)
    grad_ffn_part, grad_gate_bf, grad_up_bf, product_bf = lax.optimization_barrier(
        (grad_ffn_part, grad_gate_bf, grad_up_bf, product_bf)
    )
    grad_ffn_in = row_sums(grad_ffn_part)
    grad_hidden_ffn, grad_ffn = norm_backward(grad_ffn_in, gain_ffn, ffn_unit, ffn_factor)
    grad_hidden = upstream + grad_hidden_ffn
    grad_branch, grad_post_attn = norm_backward(
        grad_hidden, gain_post_attn, branch_unit, branch_factor
    )
    grad_branch_bf = grad_branch.astype(jnp.bfloat16)
    grad_mixed_bf = (
        contract_cols(grad_branch_bf, w_out_full).astype(jnp.bfloat16).reshape(block_rows, HQ, HD)
    )
    grad_query_rot, grad_key_window, grad_value_window = attend_back(
        query_bf, key_window, value_window, query_pos, key_pos, mixed_rows, log_total, grad_mixed_bf
    )
    back_both = jnp.zeros((halo_rows, 2 * HD), jnp.float32)
    both_halo = jnp.concatenate([grad_key_window[:W], grad_value_window[:W]], axis=1)
    for offset in range(halo_count, 0, -1):
        row_start = (halo_count - offset) * halo_rows
        piece_both = both_halo[row_start : row_start + halo_rows].astype(jnp.bfloat16)
        back_both = back_both + passed_along(piece_both, "seq", -offset).astype(jnp.float32)
    back_keys = back_both[:, :HD]
    back_values = back_both[:, HD:]
    own_keys = grad_key_window[W:]
    own_values = grad_value_window[W:]
    kept_rows = block_rows - halo_rows
    grad_key_rot = jnp.concatenate([own_keys[:kept_rows], own_keys + back_keys], axis=0)
    grad_value = jnp.concatenate([own_values[:kept_rows], own_values + back_values], axis=0)
    grad_query_raw, grad_q = norm_backward(
        unrotate(grad_query_rot, cos_table[:, None, :], sin_table[:, None, :]),
        gain_query,
        query_unit,
        query_factor,
    )
    grad_key_raw, grad_k = norm_backward(
        unrotate(grad_key_rot, cos_table, sin_table), gain_key, key_unit, key_factor
    )
    grad_query_bf = grad_query_raw.reshape(block_rows, HQ * HD).astype(jnp.bfloat16)
    grad_key_bf = grad_key_raw.astype(jnp.bfloat16)
    grad_value_bf = grad_value.astype(jnp.bfloat16)
    attn_right = jnp.concatenate([grad_query_bf, grad_key_bf, grad_value_bf], axis=1)
    grad_attn_in = contract_cols(attn_right, w_qkv)
    grad_residual, grad_attn = norm_backward(grad_attn_in, gain_attn, attn_unit, attn_factor)
    grad_tokens = grad_hidden + grad_residual
    owned = width // owners
    padded = -(-(owned + 1) // 8) * 8
    ffn_left = placed(ffn_in, owned, padded, seq_size, fsdp_size)
    down_left = placed(grad_down_bf, owned, padded, seq_size, fsdp_size)
    ffn_sums = jnp.stack(
        [
            contract_rows(left, right)
            .astype(jnp.bfloat16)
            .reshape(fsdp_size, seq_size * padded, slice_width)
            for left, right in (
                (ffn_left, grad_gate_bf),
                (ffn_left, grad_up_bf),
                (down_left, product_bf),
            )
        ],
        axis=1,
    )
    ffn_sums = ffn_sums.reshape(-1, slice_width)
    ffn_sums = lax.psum_scatter(ffn_sums, "fsdp", scatter_dimension=0, tiled=True)
    ffn_sums = lax.all_to_all(
        ffn_sums.reshape(3, seq_size, padded, slice_width), "seq", 1, 1, tiled=True
    )
    ffn_sums = (
        ffn_sums[:, :, :owned]
        .reshape(3, seq_size, owned, fsdp_size, piece)
        .transpose(0, 2, 3, 1, 4)
        .reshape(3, owned, fsdp_size * ffn_block)
        .astype(jnp.float32)
    )
    gain_grads = (grad_attn, grad_post_attn, grad_ffn, grad_post_ffn, grad_q, grad_k)
    gain_right = jnp.concatenate([part.reshape(owners, -1) for part in gain_grads], axis=1)
    attn_width = attn_right.shape[1]
    total_width = attn_width + query_width
    owner = jnp.arange(owners)
    owner_slot = ((owner % fsdp_size) * seq_size + owner // fsdp_size) * padded + owned
    gain_left = (jnp.arange(owners * padded)[None, :] == owner_slot[:, None]).astype(jnp.bfloat16)
    sum_left = jnp.concatenate(
        [
            placed(attn_in, owned, padded, seq_size, fsdp_size),
            placed(grad_branch_bf, owned, padded, seq_size, fsdp_size),
            gain_left,
        ],
        axis=0,
    )
    sum_right = jnp.concatenate(
        [
            jnp.pad(attn_right, ((0, 0), (0, query_width))),
            jnp.pad(mixed_bf, ((0, 0), (attn_width, 0))),
            jnp.pad(
                gain_right.astype(jnp.bfloat16),
                ((0, 0), (0, total_width - gain_right.shape[1])),
            ),
        ],
        axis=0,
    )
    attn_sums = lax.psum_scatter(
        contract_rows(sum_left, sum_right).astype(jnp.bfloat16),
        "fsdp",
        scatter_dimension=0,
        tiled=True,
    )
    attn_sums = lax.psum_scatter(attn_sums, "seq", scatter_dimension=0, tiled=True).astype(
        jnp.float32
    )
    gain_sums = []
    edge = 0
    for part in gain_grads:
        count = part.shape[0] // owners
        gain_sums.append(attn_sums[owned, edge : edge + count])
        edge += count
    grad_attn, grad_post_attn, grad_ffn, grad_post_ffn, grad_q, grad_k = gain_sums
    gain_sums = (grad_attn, grad_q, grad_k, grad_post_attn, grad_ffn, grad_post_ffn)
    grad_w_gate = ffn_sums[0]
    grad_w_up = ffn_sums[1]
    grad_w_down = jnp.transpose(ffn_sums[2])
    grad_w_query = attn_sums[:owned, :query_width]
    grad_w_key = attn_sums[:owned, query_width : query_width + HD]
    grad_w_value = attn_sums[:owned, query_width + HD : attn_width]
    grad_w_out = jnp.transpose(attn_sums[:owned, attn_width:])
    return (
        layer_out[None],
        grad_tokens[None],
        gain_sums[0],
        gain_sums[1],
        gain_sums[2],
        gain_sums[3],
        gain_sums[4],
        gain_sums[5],
        grad_w_query,
        grad_w_key,
        grad_w_value,
        grad_w_out,
        grad_w_gate,
        grad_w_up,
        grad_w_down,
    )


def solution(mesh):
    in_specs = (
        P("fsdp", "seq", None),
        P("fsdp", "seq", None),
        P("fsdp"),
        P("fsdp"),
        P("fsdp"),
        P("fsdp"),
        P("fsdp"),
        P("fsdp"),
        P("fsdp", None),
        P("fsdp", None),
        P("fsdp", None),
        P("fsdp", None),
        P("fsdp", None),
        P("fsdp", None),
        P("fsdp", None),
    )
    out_specs = (
        P("fsdp", "seq", None),
        P("fsdp", "seq", None),
        P(("seq", "fsdp")),
        P(("seq", "fsdp")),
        P(("seq", "fsdp")),
        P(("seq", "fsdp")),
        P(("seq", "fsdp")),
        P(("seq", "fsdp")),
        P(("seq", "fsdp"), None),
        P(("seq", "fsdp"), None),
        P(("seq", "fsdp"), None),
        P(None, ("seq", "fsdp")),
        P(("seq", "fsdp"), None),
        P(("seq", "fsdp"), None),
        P(None, ("seq", "fsdp")),
    )
    return jax.shard_map(
        on_device, mesh=mesh, in_specs=in_specs, out_specs=out_specs, check_vma=False
    )
```
